32 devices in a mesh: dp: 8 (over z, x), tensor: 4 (over y, core).
Axes of the slice: x: 2, y: 2, z: 4, core: 2. Of those that a mesh axis runs over, the one named last changes fastest.
Arguments:
- block_in: float32 [4096, 1024], P(('dp', 'tensor')), may hold values from -20 to 20
- in_proj: bfloat16 [3, 1024, 1024], P(None, 'dp', 'tensor'), may hold values from -4 to 4
- in_bias: bfloat16 [2, 16, 64], P(None, 'tensor', 'dp'), may hold values from -3 to 3
- out_proj: bfloat16 [1024, 1024], P('tensor', 'dp'), may hold values from -3 to 3
- up_proj: bfloat16 [1024, 4096], P('dp', 'tensor'), may hold values from -0.1875 to 0.1875
- up_bias: bfloat16 [16, 256], P('tensor', 'dp'), may hold values from -3 to 3
- down_proj: bfloat16 [4096, 1024], P('tensor', 'dp'), may hold values from -0.1875 to 0.1875
- norm_params: bfloat16 [6, 1024], P(None, 'dp'), may hold values from -2 to 2
- grad_out: float32 [4096, 1024], P(('dp', 'tensor')), may hold values from -6 to 6
Outputs:
- block_out: float32 [4096, 1024], P(('dp', 'tensor'))
- grad_in: float32 [4096, 1024], P(('dp', 'tensor'))
- grad_in_proj: float32 [3, 1024, 1024], P(None, 'dp', 'tensor')
- grad_in_bias: float32 [2, 16, 64], P(None, 'tensor', 'dp')
- grad_out_proj: float32 [1024, 1024], P('tensor', 'dp')
- grad_up_proj: float32 [1024, 4096], P('dp', 'tensor')
- grad_up_bias: float32 [16, 256], P('tensor', 'dp')
- grad_down_proj: float32 [4096, 1024], P('tensor', 'dp')
- grad_norm_params: float32 [6, 1024], P(None, ('dp', 'tensor'))
The draws below stay inside these ranges and needn't reach their ends.
All inputs are finite; a program needn't handle non-finite values.
Results may differ from the reference program's by a relative error of at most 0.015.
The reference program's roundings to bfloat16 on the way count: a program that leaves them out, or rounds other values in their place, can miss the bound.
Values may be sent and summed in bfloat16 or wider, within the bound.
A program may use at most 128 MiB of HBM per device.

```python
import math
import jax
import jax.numpy as jnp
from jax import lax

D = 1024
H = 16
HD = 64
FF = 4096
LEN = 512
TOKENS = 4096
N_DP = 8


def draw_block_in(key, part):
    key_a = jax.random.fold_in(key, 11)
    key_b = jax.random.fold_in(key, 12)
    key_c = jax.random.fold_in(key, 13)
    row_scale = jnp.exp(jax.random.uniform(key_b, (TOKENS, 1), jnp.float32, math.log(1.0), math.log(4.0)))
    col_scale = jnp.exp(jax.random.uniform(key_c, (1, D), jnp.float32, math.log(0.7), math.log(1.4)))
    noise = jax.random.normal(key_a, (TOKENS, D), jnp.float32)
    value = noise * row_scale * col_scale
    return jnp.clip(value, -20.0, 20.0).astype(jnp.float32)


def draw_in_proj(key, part):
    key_a = jax.random.fold_in(key, 21)
    base = jax.random.normal(key_a, (3, D, D), jnp.float32) * (1.0 / math.sqrt(D))
    return jnp.clip(base, -4.0, 4.0).astype(jnp.bfloat16)


def draw_norm_params(key, part):
    noise = jax.random.normal(jax.random.fold_in(key, 31), (6, D), jnp.float32)
    row_ids = jnp.arange(6, dtype=jnp.int32)[:, None]
    is_gain = (row_ids == 0) | (row_ids == 3)
    value = jnp.where(is_gain, 1.0 + 0.12 * noise, 0.3 * noise)
    return jnp.clip(value, -2.0, 2.0).astype(jnp.bfloat16)


def raised(array, rng, source, target, shards_of, factor):
    def block_of(axis_at):
        return (jnp.arange(array.shape[axis_at]) // (array.shape[axis_at] // shards_of)).reshape((-1,) + (1,) * (array.ndim - 1 - axis_at))

    first = jax.random.permutation(rng, shards_of)[block_of(target)]
    far = (block_of(target) + shards_of // 2) % shards_of
    return jnp.where((block_of(source) == first) | (block_of(source) == far), factor * array, array)


def steps_of(rng, extent, split, low, top_value):
    loudness, own = 1.0, jax.random.fold_in(rng, 6)
    for axis_at, blocks in split:
        heights = jnp.exp(jax.random.uniform(jax.random.fold_in(own, axis_at), (blocks,), jnp.float32, low / len(split), top_value / len(split)))
        loudness = loudness * jnp.repeat(heights, extent[axis_at] // blocks).reshape([-1 if axis == axis_at else 1 for axis in range(len(extent))])
    return loudness


def bell_draw(rng, shape, width, bound, cuts=(), held_as=jnp.bfloat16):
    drawn = width * jax.random.normal(rng, shape, jnp.float32)
    if cuts:
        drawn = drawn * steps_of(rng, shape, cuts, -0.22, 0.18)
    return jnp.clip(drawn, -bound, bound).astype(held_as)


def bell_draw_with(stream_key, extent, width, most, pieces, heavy, held_as=jnp.bfloat16):
    array = width * jax.random.normal(stream_key, extent, jnp.float32)
    if pieces:
        array = array * steps_of(stream_key, extent, pieces, -0.22, 0.18)
    return jnp.clip(raised(array, jax.random.fold_in(stream_key, 3), *heavy), -most, most).astype(held_as)


def setup_inputs(seed: int = 0) -> dict:
    arg_keys = jax.random.split(jax.random.key(seed), 10)
    block_in = draw_block_in(jax.random.fold_in(arg_keys[9], 71), 0)
    in_proj = draw_in_proj(jax.random.fold_in(arg_keys[9], 71), 0)
    in_bias = bell_draw(arg_keys[2], (2, H, HD), 0.5, 3.0, ((1, 4), (2, 8)))
    out_proj = bell_draw(arg_keys[3], (D, D), (max(2 * D // LEN, 1)) ** -0.5, 3.0, ((0, 4), (1, 8)))
    up_proj = bell_draw(arg_keys[4], (D, FF), D ** -0.5, 0.1875, ((0, 8), (1, 4)))
    up_bias = bell_draw(arg_keys[5], (H, FF // H), 0.5, 3.0, ((0, 4), (1, 8)))
    down_proj = bell_draw(arg_keys[6], (FF, D), (FF // 4) ** -0.5, 0.1875, ((0, 4), (1, 8)))
    norm_params = draw_norm_params(jax.random.fold_in(arg_keys[9], 71), 0)
    grad_out = bell_draw_with(arg_keys[8], (TOKENS, D), 1.0, 6.0, ((0, 32),), (0, 1, 32, 2.75), jnp.float32)
    return {"block_in": block_in, "in_proj": in_proj, "in_bias": in_bias, "out_proj": out_proj, "up_proj": up_proj, "up_bias": up_bias, "down_proj": down_proj, "norm_params": norm_params, "grad_out": grad_out}


def layer_norm(rows, gain, shift):
    center = rows - lax.optimization_barrier(jnp.mean(rows, -1, keepdims=True))
    var = lax.optimization_barrier(jnp.mean(center * center, -1, keepdims=True))
    return center * lax.rsqrt(var + 1e-05) * gain + shift

def gelu_curve(value):
    return 0.5 * value * (1.0 + jnp.tanh(0.7978845608 * (value + 0.044715 * value * value * value)))

def block_scores(rows_q, keys, start, scale, seq_len):
    block_rows = rows_q.shape[0]
    scores = jnp.einsum('qhe,khe->hqk', rows_q.astype(jnp.float32), keys.astype(jnp.float32)) * scale
    positions = start + jnp.arange(block_rows, dtype=jnp.int32)
    allowed = jnp.arange(seq_len, dtype=jnp.int32)[None, :] <= positions[:, None]
    return (jnp.where(allowed[None], scores, -1e+30), allowed)

def attend(query, keys, values):
    seq_len, heads, head_dim = query.shape
    block_rows = min(512, seq_len)
    count = seq_len // block_rows
    scale = 1.0 / math.sqrt(head_dim)
    starts = jnp.arange(count, dtype=jnp.int32) * block_rows

    def one_block(item):
        rows_q, start = item
        scores, allowed = block_scores(rows_q, keys, start, scale, seq_len)
        peak = lax.optimization_barrier(jnp.max(scores, -1, keepdims=True))
        expo = jnp.exp(scores - peak)
        total = lax.optimization_barrier(jnp.sum(expo, -1, keepdims=True))
        probs = (expo / total).astype(jnp.bfloat16)
        out = jnp.einsum('hqk,khe->qhe', probs.astype(jnp.float32), values.astype(jnp.float32)).astype(jnp.bfloat16)
        return (out, (peak + jnp.log(total))[:, :, 0])
    outs, logs = lax.map(one_block, (query.reshape(count, block_rows, heads, head_dim), starts))
    return (outs.reshape(seq_len, heads, head_dim), logs)

def attend_back(query, keys, values, mixed, grad_mixed, log_total):
    seq_len, heads, head_dim = query.shape
    block_rows = min(512, seq_len)
    count = seq_len // block_rows
    scale = 1.0 / math.sqrt(head_dim)
    starts = jnp.arange(count, dtype=jnp.int32) * block_rows
    row_dot = lax.optimization_barrier(jnp.sum(grad_mixed.astype(jnp.float32) * mixed.astype(jnp.float32), -1))
    keys_f = keys.astype(jnp.float32)
    values_f = values.astype(jnp.float32)

    def step(carry, item):
        grad_k, grad_v = carry
        rows_q, rows_g, rows_log, rows_dot, start = item
        scores, allowed = block_scores(rows_q, keys, start, scale, seq_len)
        probs = jnp.where(allowed[None], jnp.exp(scores - rows_log[:, :, None]), 0.0)
        probs_low = probs.astype(jnp.bfloat16).astype(jnp.float32)
        grad_g = rows_g.astype(jnp.float32)
        grad_v = grad_v + jnp.einsum('hqk,qhe->khe', probs_low, grad_g)
        grad_p = jnp.einsum('qhe,khe->hqk', grad_g, values_f)
        grad_s = (probs * (grad_p - jnp.transpose(rows_dot)[:, :, None])).astype(jnp.bfloat16).astype(jnp.float32)
        grad_q = jnp.einsum('hqk,khe->qhe', grad_s, keys_f) * scale
        grad_k = grad_k + jnp.einsum('hqk,qhe->khe', grad_s, rows_q.astype(jnp.float32)) * scale
        return ((grad_k, grad_v), grad_q)
    zeros = jnp.zeros((seq_len, heads, head_dim), jnp.float32)
    items = (query.reshape(count, block_rows, heads, head_dim), grad_mixed.reshape(count, block_rows, heads, head_dim), log_total, row_dot.reshape(count, block_rows, heads), starts)
    (grad_k, grad_v), grad_qs = lax.scan(step, (zeros, zeros), items)
    return (grad_qs.reshape(seq_len, heads, head_dim), grad_k, grad_v)

def reference(block_in, in_proj, in_bias, out_proj, up_proj, up_bias, down_proj, norm_params, grad_out):
    norms = norm_params.astype(jnp.float32)
    gain_one, shift_one, bias_attn, gain_two, shift_two, bias_feed = [norms[i] for i in range(6)]
    bias_flat = in_bias.astype(jnp.float32).reshape(2, D)
    bias_up = up_bias.astype(jnp.float32).reshape(FF)
    proj_f = in_proj.astype(jnp.float32)

    def one_sequence(carry, item):
        seq_in, seq_grad = item
        normed_one = layer_norm(seq_in, gain_one, shift_one).astype(jnp.bfloat16)
        projected = jnp.einsum('ld,jdc->jlc', normed_one.astype(jnp.float32), proj_f)
        query = (projected[0] + bias_flat[0]).astype(jnp.bfloat16).reshape(LEN, H, HD)
        keys = projected[1].astype(jnp.bfloat16).reshape(LEN, H, HD)
        values = (projected[2] + bias_flat[1]).astype(jnp.bfloat16).reshape(LEN, H, HD)
        mixed, log_total = attend(query, keys, values)
        mixed_flat = mixed.reshape(LEN, D)
        middle = seq_in + jnp.dot(mixed_flat, out_proj, preferred_element_type=jnp.float32) + bias_attn
        normed_two = layer_norm(middle, gain_two, shift_two).astype(jnp.bfloat16)
        hidden_pre = jnp.dot(normed_two, up_proj, preferred_element_type=jnp.float32) + bias_up
        hidden = gelu_curve(hidden_pre).astype(jnp.bfloat16)
        seq_out = middle + jnp.dot(hidden, down_proj, preferred_element_type=jnp.float32) + bias_feed
        grad_low = seq_grad.astype(jnp.bfloat16)
        grad_down = jnp.dot(hidden.T, grad_low, preferred_element_type=jnp.float32)
        grad_hidden = jnp.dot(grad_low, down_proj.T, preferred_element_type=jnp.float32)
        _, curve_back = jax.vjp(gelu_curve, hidden_pre)
        grad_pre = curve_back(grad_hidden)[0]
        grad_upb = lax.optimization_barrier(jnp.sum(grad_pre, 0)).reshape(H, FF // H)
        grad_pre_low = grad_pre.astype(jnp.bfloat16)
        grad_up = jnp.dot(normed_two.T, grad_pre_low, preferred_element_type=jnp.float32)
        normed_two_grad = jnp.dot(grad_pre_low, up_proj.T, preferred_element_type=jnp.float32)
        _, norm_back_two = jax.vjp(layer_norm, middle, gain_two, shift_two)
        grad_mid_norm, grad_gain_two, grad_shift_two = norm_back_two(normed_two_grad)
        grad_middle = seq_grad + grad_mid_norm
        middle_low = grad_middle.astype(jnp.bfloat16)
        grad_proj_out = jnp.dot(mixed_flat.T, middle_low, preferred_element_type=jnp.float32)
        grad_mixed = jnp.dot(middle_low, out_proj.T, preferred_element_type=jnp.float32).astype(jnp.bfloat16).reshape(LEN, H, HD)
        grad_q, grad_k, grad_v = attend_back(query, keys, values, mixed, grad_mixed, log_total)
        grad_bias_in = jnp.stack([lax.optimization_barrier(jnp.sum(grad_q, 0)), lax.optimization_barrier(jnp.sum(grad_v, 0))])
        grad_proj = jnp.stack([grad_q, grad_k, grad_v]).reshape(3, LEN, D).astype(jnp.bfloat16).astype(jnp.float32)
        grad_in_w = jnp.einsum('ld,jlc->jdc', normed_one.astype(jnp.float32), grad_proj)
        normed_one_grad = jnp.einsum('jlc,jdc->ld', grad_proj, proj_f)
        _, norm_back_one = jax.vjp(layer_norm, seq_in, gain_one, shift_one)
        grad_in_norm, grad_gain_one, grad_shift_one = norm_back_one(normed_one_grad)
        seq_grad_in = grad_middle + grad_in_norm
        norm_terms = jnp.stack([grad_gain_one, grad_shift_one, lax.optimization_barrier(jnp.sum(grad_middle, 0)), grad_gain_two, grad_shift_two, lax.optimization_barrier(jnp.sum(seq_grad, 0))])
        terms = (grad_in_w, grad_bias_in, grad_proj_out, grad_up, grad_upb, grad_down, norm_terms)
        return (tuple((a + b for a, b in zip(carry, terms))), (seq_out, seq_grad_in))
    init = (jnp.zeros((3, D, D), jnp.float32), jnp.zeros((2, H, HD), jnp.float32), jnp.zeros((D, D), jnp.float32), jnp.zeros((D, FF), jnp.float32), jnp.zeros((H, FF // H), jnp.float32), jnp.zeros((FF, D), jnp.float32), jnp.zeros((6, D), jnp.float32))
    sums, (outs, grads) = lax.scan(one_sequence, init, (block_in.reshape(N_DP, LEN, D), grad_out.reshape(N_DP, LEN, D)))
    return (outs.reshape(TOKENS, D), grads.reshape(TOKENS, D), sums[0], sums[1], sums[2], sums[3], sums[4], sums[5], sums[6])
```

```python
import functools
import math

import jax
import jax.numpy as jnp
from jax import lax
from jax.experimental import pallas as pl
from jax.experimental.pallas import tpu as pltpu
from jax.sharding import PartitionSpec as P

MESH = pl.DeviceIdType.MESH


def greet(axis, peers):
    barrier = pltpu.get_barrier_semaphore()
    for peer in peers:
        pl.semaphore_signal(barrier, inc=1, device_id={axis: peer}, device_id_type=MESH)
    pl.semaphore_wait(barrier, len(peers))


def send(axis, src, dst, send_sem, recv_sem, peer):
    return pltpu.make_async_remote_copy(
        src_ref=src,
        dst_ref=dst,
        send_sem=send_sem,
        recv_sem=recv_sem,
        device_id={axis: peer},
        device_id_type=MESH,
    )


def gather_kernel(axis, n, x_ref, out_ref, send_sem, recv_sem, own_sem):
    me = lax.axis_index(axis)
    groups = n // 2
    side, group = lax.rem(me, 2), me // 2
    mate = group * 2 + 1 - side
    across = [lax.rem(group + k, groups) * 2 + side for k in range(1, groups)]
    behind = [lax.rem(group + groups - k, groups) * 2 + side for k in range(1, groups)]
    greet(axis, [mate] + across)
    own = pltpu.make_async_copy(x_ref, out_ref.at[me], own_sem)
    own.start()
    far = []
    for k, peer in enumerate(across):
        far.append(send(axis, x_ref, out_ref.at[me], send_sem.at[k], recv_sem.at[k], peer))
        far[-1].start()
    near = [send(axis, x_ref, out_ref.at[me], send_sem.at[groups], recv_sem.at[groups], mate)]
    near[0].start()
    for k, copy in enumerate(far):
        copy.wait_recv()
        at = groups + 1 + k
        block = out_ref.at[behind[k]]
        near.append(send(axis, block, block, send_sem.at[at], recv_sem.at[at], mate))
        near[-1].start()
    for copy in far:
        copy.wait_send()
    for copy in near:
        copy.wait()
    own.wait()


def gather_rows(x, axis, n, collective_id):
    rows, columns = x.shape
    out = pl.pallas_call(
        functools.partial(gather_kernel, axis, n),
        out_shape=jax.ShapeDtypeStruct((n, rows, columns), x.dtype),
        in_specs=[pl.BlockSpec(memory_space=pltpu.VMEM)],
        out_specs=pl.BlockSpec(memory_space=pltpu.VMEM),
        scratch_shapes=[
            pltpu.SemaphoreType.DMA((n,)),
            pltpu.SemaphoreType.DMA((n,)),
            pltpu.SemaphoreType.DMA,
        ],
        compiler_params=pltpu.CompilerParams(collective_id=collective_id, has_side_effects=True),
    )(x)
    return out.reshape(n * rows, columns)


def scatter_kernel(axis, n, x_ref, out_ref, got, mine, far_got, send_sem, recv_sem):
    me = lax.axis_index(axis)
    groups = n // 2
    side, group = lax.rem(me, 2), me // 2
    mate = group * 2 + 1 - side
    across = [lax.rem(group + k, groups) * 2 + side for k in range(1, groups)]
    greet(axis, [mate] + across)
    near = []
    for k in range(1, groups + 1):
        there = lax.rem(group + k, groups)
        block = x_ref.at[there * 2 + 1 - side]
        near.append(send(axis, block, got.at[k - 1], send_sem.at[k - 1], recv_sem.at[k - 1], mate))
        near[-1].start()
    far = []
    for k in range(1, groups):
        near[k - 1].wait_recv()
        there = lax.rem(group + k, groups)
        both = x_ref[there * 2 + side].astype(jnp.float32) + got[k - 1].astype(jnp.float32)
        mine[k - 1] = both.astype(mine.dtype)
        at = groups + k
        far.append(
            send(axis, mine.at[k - 1], far_got.at[k - 1], send_sem.at[at], recv_sem.at[at], across[k - 1])
        )
        far[-1].start()
    near[groups - 1].wait_recv()
    out_ref[...] = x_ref[me].astype(jnp.float32) + got[groups - 1].astype(jnp.float32)
    for k, copy in enumerate(far):
        copy.wait_recv()
        out_ref[...] += far_got[k].astype(jnp.float32)
    for copy in near + far:
        copy.wait_send()


def scatter_rows(x, axis, n, collective_id):
    rows, columns = x.shape
    rows = rows // n
    groups = n // 2
    return pl.pallas_call(
        functools.partial(scatter_kernel, axis, n),
        out_shape=jax.ShapeDtypeStruct((rows, columns), jnp.float32),
        in_specs=[pl.BlockSpec(memory_space=pltpu.VMEM)],
        out_specs=pl.BlockSpec(memory_space=pltpu.VMEM),
        scratch_shapes=[
            pltpu.VMEM((groups, rows, columns), jnp.bfloat16),
            pltpu.VMEM((max(groups - 1, 1), rows, columns), jnp.bfloat16),
            pltpu.VMEM((max(groups - 1, 1), rows, columns), jnp.bfloat16),
            pltpu.SemaphoreType.DMA((n,)),
            pltpu.SemaphoreType.DMA((n,)),
        ],
        compiler_params=pltpu.CompilerParams(collective_id=collective_id, has_side_effects=True),
    )(x.astype(jnp.bfloat16).reshape(n, rows, columns))


def exchange_kernel(axis, n, whole, x_ref, out_ref, send_sem, recv_sem, own_sem):
    me = lax.axis_index(axis)
    peers = [lax.rem(me + k, n) for k in range(1, n)]
    greet(axis, peers)
    own = pltpu.make_async_copy(x_ref if whole else x_ref.at[me], out_ref.at[me], own_sem)
    own.start()
    copies = []
    for k, peer in enumerate(peers):
        src = x_ref if whole else x_ref.at[peer]
        copies.append(send(axis, src, out_ref.at[me], send_sem.at[k], recv_sem.at[k], peer))
        copies[-1].start()
    for copy in copies:
        copy.wait()
    own.wait()


def exchange(x, axis, n, collective_id, whole):
    block = x.shape if whole else x.shape[1:]
    return pl.pallas_call(
        functools.partial(exchange_kernel, axis, n, whole),
        out_shape=jax.ShapeDtypeStruct((n,) + block, x.dtype),
        in_specs=[pl.BlockSpec(memory_space=pltpu.VMEM)],
        out_specs=pl.BlockSpec(memory_space=pltpu.VMEM),
        scratch_shapes=[
            pltpu.SemaphoreType.DMA((n,)),
            pltpu.SemaphoreType.DMA((n,)),
            pltpu.SemaphoreType.DMA,
        ],
        compiler_params=pltpu.CompilerParams(collective_id=collective_id, has_side_effects=True),
    )(x)


def packed(parts, lead):
    flat = jnp.concatenate([p.reshape(lead + (-1,)) for p in parts], -1)
    size = flat.shape[-1]
    room = -(-size // 2048) * 2048
    flat = jnp.pad(flat, [(0, 0)] * len(lead) + [(0, room - size)])
    return flat.reshape(lead + (room // 128, 128))


def layer_norm(rows, gain, shift):
    center = rows - jnp.mean(rows, -1, keepdims=True)
    var = jnp.mean(center * center, -1, keepdims=True)
    return center * lax.rsqrt(var + 1e-05) * gain + shift


def gelu_curve(value):
    return 0.5 * value * (1.0 + jnp.tanh(0.7978845608 * (value + 0.044715 * value * value * value)))


def block_scores(rows_q, keys, start, scale, seq_len):
    block_rows = rows_q.shape[0]
    scores = jnp.einsum("qhe,khe->hqk", rows_q, keys, preferred_element_type=jnp.float32) * scale
    positions = start + jnp.arange(block_rows, dtype=jnp.int32)
    allowed = jnp.arange(seq_len, dtype=jnp.int32)[None, :] <= positions[:, None]
    return (jnp.where(allowed[None], scores, -1e30), allowed)


def attend(query, keys, values):
    seq_len, heads, head_dim = query.shape
    block_rows = min(512, seq_len)
    count = seq_len // block_rows
    scale = 1.0 / math.sqrt(head_dim)
    starts = jnp.arange(count, dtype=jnp.int32) * block_rows

    def one_block(item):
        rows_q, start = item
        scores, allowed = block_scores(rows_q, keys, start, scale, seq_len)
        peak = jnp.max(scores, -1, keepdims=True)
        expo = jnp.exp(scores - peak)
        total = jnp.sum(expo, -1, keepdims=True)
        probs = (expo / total).astype(jnp.bfloat16)
        out = jnp.einsum("hqk,khe->qhe", probs, values, preferred_element_type=jnp.float32).astype(
            jnp.bfloat16
        )
        return (out, (peak + jnp.log(total))[:, :, 0])

    outs, logs = lax.map(one_block, (query.reshape(count, block_rows, heads, head_dim), starts))
    return (outs.reshape(seq_len, heads, head_dim), logs)


def attend_back(query, keys, values, mixed, grad_mixed, log_total):
    seq_len, heads, head_dim = query.shape
    block_rows = min(512, seq_len)
    count = seq_len // block_rows
    scale = 1.0 / math.sqrt(head_dim)
    starts = jnp.arange(count, dtype=jnp.int32) * block_rows
    row_dot = jnp.sum(grad_mixed.astype(jnp.float32) * mixed.astype(jnp.float32), -1)

    def step(carry, item):
        grad_k, grad_v = carry
        rows_q, rows_g, rows_log, rows_dot, start = item
        scores, allowed = block_scores(rows_q, keys, start, scale, seq_len)
        probs = jnp.where(allowed[None], jnp.exp(scores - rows_log[:, :, None]), 0.0)
        probs_low = probs.astype(jnp.bfloat16)
        grad_v = grad_v + jnp.einsum(
            "hqk,qhe->khe", probs_low, rows_g, preferred_element_type=jnp.float32
        )
        grad_p = jnp.einsum("qhe,khe->hqk", rows_g, values, preferred_element_type=jnp.float32)
        grad_s = (probs * (grad_p - jnp.transpose(rows_dot)[:, :, None])).astype(jnp.bfloat16)
        grad_q = (
            jnp.einsum("hqk,khe->qhe", grad_s, keys, preferred_element_type=jnp.float32) * scale
        )
        grad_k = (
            grad_k
            + jnp.einsum("hqk,qhe->khe", grad_s, rows_q, preferred_element_type=jnp.float32) * scale
        )
        return ((grad_k, grad_v), grad_q)

    zeros = jnp.zeros((seq_len, heads, head_dim), jnp.float32)
    items = (
        query.reshape(count, block_rows, heads, head_dim),
        grad_mixed.reshape(count, block_rows, heads, head_dim),
        log_total,
        row_dot.reshape(count, block_rows, heads),
        starts,
    )
    (grad_k, grad_v), grad_qs = lax.scan(step, (zeros, zeros), items)
    return (grad_qs.reshape(seq_len, heads, head_dim), grad_k, grad_v)


def body(dp, tensor, block_in, in_proj, in_bias, out_proj, up_proj, up_bias, down_proj, norm_params, grad_out):
    proj_in = lax.all_gather(in_proj, "dp", axis=1, tiled=True)
    proj_out = lax.all_gather(out_proj, "dp", axis=1, tiled=True)
    small = exchange(packed([norm_params, in_bias, up_bias], ()), "dp", dp, 0, True)
    small = small.reshape(dp, -1)
    ends = [norm_params.size, norm_params.size + in_bias.size]
    ends.append(ends[1] + up_bias.size)
    norms = small[:, : ends[0]].reshape((dp,) + norm_params.shape)
    norms = norms.transpose(1, 0, 2).reshape(6, -1)
    bias_in = small[:, ends[0] : ends[1]].reshape((dp,) + in_bias.shape)
    bias_in = bias_in.transpose(1, 2, 0, 3).reshape(2, in_bias.shape[1], -1)
    bias_up = small[:, ends[1] : ends[2]].reshape((dp,) + up_bias.shape)
    bias_up = bias_up.transpose(1, 0, 2).reshape(up_bias.shape[0], -1)
    norms = norms.astype(jnp.float32)
    gain_one, shift_one, bias_attn, gain_two, shift_two, bias_feed = [norms[i] for i in range(6)]
    heads_here = bias_in.shape[1]
    head_dim = bias_in.shape[2]
    columns = heads_here * head_dim
    normed_one = layer_norm(block_in, gain_one, shift_one).astype(jnp.bfloat16)
    whole_one = gather_rows(normed_one, "tensor", tensor, 1)
    seq_len = whole_one.shape[0]
    projected = jnp.einsum("ld,jdc->jlc", whole_one, proj_in, preferred_element_type=jnp.float32)
    bias_flat = bias_in.astype(jnp.float32).reshape(2, columns)
    query = (
        (projected[0] + bias_flat[0]).astype(jnp.bfloat16).reshape(seq_len, heads_here, head_dim)
    )
    keys = projected[1].astype(jnp.bfloat16).reshape(seq_len, heads_here, head_dim)
    values = (
        (projected[2] + bias_flat[1]).astype(jnp.bfloat16).reshape(seq_len, heads_here, head_dim)
    )
    mixed, log_total = attend(query, keys, values)
    mixed_flat = mixed.reshape(seq_len, columns)
    attn_part = jnp.dot(mixed_flat, proj_out, preferred_element_type=jnp.float32)
    attn_sum = scatter_rows(attn_part, "tensor", tensor, 5)
    middle = block_in + attn_sum + bias_attn
    normed_two = layer_norm(middle, gain_two, shift_two).astype(jnp.bfloat16)
    whole_two = gather_rows(normed_two, "tensor", tensor, 2)
    proj_up = lax.all_gather(up_proj, "dp", axis=0, tiled=True)
    proj_down = lax.all_gather(down_proj, "dp", axis=1, tiled=True)
    hidden_pre = jnp.dot(whole_two, proj_up, preferred_element_type=jnp.float32) + bias_up.astype(
        jnp.float32
    ).reshape(-1)
    hidden = gelu_curve(hidden_pre).astype(jnp.bfloat16)
    feed_part = jnp.dot(hidden, proj_down, preferred_element_type=jnp.float32)
    feed_sum = scatter_rows(feed_part, "tensor", tensor, 6)
    block_out = middle + feed_sum + bias_feed
    grad_low = grad_out.astype(jnp.bfloat16)
    whole_grad = gather_rows(grad_low, "tensor", tensor, 3)
    grad_down = jnp.einsum("lf,ld->fd", hidden, whole_grad, preferred_element_type=jnp.float32)
    grad_hidden = jnp.einsum("ld,fd->lf", whole_grad, proj_down, preferred_element_type=jnp.float32)
    _, curve_back = jax.vjp(gelu_curve, hidden_pre)
    grad_pre = curve_back(grad_hidden)[0]
    grad_upb = jnp.sum(grad_pre, 0).reshape(bias_up.shape)
    grad_pre_low = grad_pre.astype(jnp.bfloat16)
    grad_up = jnp.einsum("ld,lf->df", whole_two, grad_pre_low, preferred_element_type=jnp.float32)
    two_part = jnp.einsum("lf,df->ld", grad_pre_low, proj_up, preferred_element_type=jnp.float32)
    normed_two_grad = scatter_rows(two_part, "tensor", tensor, 7)
    _, norm_back_two = jax.vjp(layer_norm, middle, gain_two, shift_two)
    grad_mid_norm, grad_gain_two, grad_shift_two = norm_back_two(normed_two_grad)
    grad_middle = grad_out + grad_mid_norm
    middle_low = grad_middle.astype(jnp.bfloat16)
    whole_mid = gather_rows(middle_low, "tensor", tensor, 4)
    grad_proj_out = jnp.einsum(
        "lc,ld->cd", mixed_flat, whole_mid, preferred_element_type=jnp.float32
    )
    grad_mixed = jnp.einsum("ld,cd->lc", whole_mid, proj_out, preferred_element_type=jnp.float32)
    grad_mixed = grad_mixed.astype(jnp.bfloat16).reshape(seq_len, heads_here, head_dim)
    grad_q, grad_k, grad_v = attend_back(query, keys, values, mixed, grad_mixed, log_total)
    grad_bias_in = jnp.stack([jnp.sum(grad_q, 0), jnp.sum(grad_v, 0)])
    grad_proj = (
        jnp.stack([grad_q, grad_k, grad_v]).reshape(3, seq_len, columns).astype(jnp.bfloat16)
    )
    grad_in_w = jnp.einsum("ld,jlc->jdc", whole_one, grad_proj, preferred_element_type=jnp.float32)
    one_part = jnp.einsum("jlc,jdc->ld", grad_proj, proj_in, preferred_element_type=jnp.float32)
    normed_one_grad = scatter_rows(one_part, "tensor", tensor, 8)
    _, norm_back_one = jax.vjp(layer_norm, block_in, gain_one, shift_one)
    grad_in_norm, grad_gain_one, grad_shift_one = norm_back_one(normed_one_grad)
    grad_in = grad_middle + grad_in_norm
    norm_terms = jnp.stack(
        [
            grad_gain_one,
            grad_shift_one,
            jnp.sum(grad_middle, 0),
            grad_gain_two,
            grad_shift_two,
            jnp.sum(grad_out, 0),
        ]
    )
    pieces = [
        norm_terms.reshape(6, dp, -1).transpose(1, 0, 2),
        grad_bias_in.reshape(in_bias.shape[:2] + (dp, -1)).transpose(2, 0, 1, 3),
        grad_upb.reshape(up_bias.shape[0], dp, -1).transpose(1, 0, 2),
    ]
    pieces = [p.reshape(dp, -1) for p in pieces]
    tiny = jnp.sum(exchange(packed(pieces, (dp,)), "dp", dp, 9, False), 0).reshape(-1)
    grad_in_bias = tiny[ends[0] : ends[1]].reshape(in_bias.shape)
    grad_up_bias = tiny[ends[1] : ends[2]].reshape(up_bias.shape)
    quarter = tiny[: ends[0]].reshape(6, tensor, -1).transpose(1, 0, 2).reshape(tensor, -1)
    width = quarter.shape[1]
    quarter = jnp.sum(exchange(packed([quarter], (tensor,)), "tensor", tensor, 10, False), 0)
    grad_norms = quarter.reshape(-1)[:width].reshape(6, -1)

    def summed(array, axis):
        return lax.psum_scatter(
            array.astype(jnp.bfloat16), "dp", scatter_dimension=axis, tiled=True
        ).astype(jnp.float32)

    grad_in_proj = summed(grad_in_w, 1)
    grad_out_proj = summed(grad_proj_out, 1)
    grad_up_proj = summed(grad_up, 0)
    grad_down_proj = summed(grad_down, 1)
    return (
        block_out,
        grad_in,
        grad_in_proj,
        grad_in_bias,
        grad_out_proj,
        grad_up_proj,
        grad_up_bias,
        grad_down_proj,
        grad_norms,
    )


def solution(mesh):
    return jax.shard_map(
        functools.partial(body, mesh.shape["dp"], mesh.shape["tensor"]),
        mesh=mesh,
        in_specs=(
            P(("dp", "tensor"), None),
            P(None, "dp", "tensor"),
            P(None, "tensor", "dp"),
            P("tensor", "dp"),
            P("dp", "tensor"),
            P("tensor", "dp"),
            P("tensor", "dp"),
            P(None, "dp"),
            P(("dp", "tensor"), None),
        ),
        out_specs=(
            P(("dp", "tensor"), None),
            P(("dp", "tensor"), None),
            P(None, "dp", "tensor"),
            P(None, "tensor", "dp"),
            P("tensor", "dp"),
            P("dp", "tensor"),
            P("tensor", "dp"),
            P("tensor", "dp"),
            P(None, ("dp", "tensor")),
        ),
        check_vma=False,
    )
```

```python
import functools
import math

import jax
import jax.numpy as jnp
from jax import lax
from jax.experimental import pallas as pl
from jax.experimental.pallas import tpu as pltpu
from jax.sharding import PartitionSpec as P

MESH = pl.DeviceIdType.MESH


def greet(axis, peers):
    barrier = pltpu.get_barrier_semaphore()
    for peer in peers:
        pl.semaphore_signal(barrier, inc=1, device_id={axis: peer}, device_id_type=MESH)
    pl.semaphore_wait(barrier, len(peers))


def send(axis, src, dst, send_sem, recv_sem, peer):
    return pltpu.make_async_remote_copy(
        src_ref=src,
        dst_ref=dst,
        send_sem=send_sem,
        recv_sem=recv_sem,
        device_id={axis: peer},
        device_id_type=MESH,
    )


def gather_kernel(axis, n, x_ref, out_ref, send_sem, recv_sem, own_sem):
    me = lax.axis_index(axis)
    groups = n // 2
    side, group = lax.rem(me, 2), me // 2
    mate = group * 2 + 1 - side
    across = [lax.rem(group + k, groups) * 2 + side for k in range(1, groups)]
    behind = [lax.rem(group + groups - k, groups) * 2 + side for k in range(1, groups)]
    greet(axis, [mate] + across)
    own = pltpu.make_async_copy(x_ref, out_ref.at[me], own_sem)
    own.start()
    far = []
    for k, peer in enumerate(across):
        far.append(send(axis, x_ref, out_ref.at[me], send_sem.at[k], recv_sem.at[k], peer))
        far[-1].start()
    near = [send(axis, x_ref, out_ref.at[me], send_sem.at[groups], recv_sem.at[groups], mate)]
    near[0].start()
    for k, copy in enumerate(far):
        copy.wait_recv()
        at = groups + 1 + k
        block = out_ref.at[behind[k]]
        near.append(send(axis, block, block, send_sem.at[at], recv_sem.at[at], mate))
        near[-1].start()
    for copy in far:
        copy.wait_send()
    for copy in near:
        copy.wait()
    own.wait()


def gather_rows(x, axis, n, collective_id):
    rows, columns = x.shape
    out = pl.pallas_call(
        functools.partial(gather_kernel, axis, n),
        out_shape=jax.ShapeDtypeStruct((n, rows, columns), x.dtype),
        in_specs=[pl.BlockSpec(memory_space=pltpu.VMEM)],
        out_specs=pl.BlockSpec(memory_space=pltpu.VMEM),
        scratch_shapes=[
            pltpu.SemaphoreType.DMA((n,)),
            pltpu.SemaphoreType.DMA((n,)),
            pltpu.SemaphoreType.DMA,
        ],
        compiler_params=pltpu.CompilerParams(collective_id=collective_id, has_side_effects=True),
    )(x)
    return out.reshape(n * rows, columns)


def scatter_kernel(axis, n, x_ref, out_ref, got, mine, far_got, send_sem, recv_sem):
    me = lax.axis_index(axis)
    groups = n // 2
    side, group = lax.rem(me, 2), me // 2
    mate = group * 2 + 1 - side
    across = [lax.rem(group + k, groups) * 2 + side for k in range(1, groups)]
    greet(axis, [mate] + across)
    near = []
    for k in range(1, groups + 1):
        there = lax.rem(group + k, groups)
        block = x_ref.at[there * 2 + 1 - side]
        near.append(send(axis, block, got.at[k - 1], send_sem.at[k - 1], recv_sem.at[k - 1], mate))
        near[-1].start()
    far = []
    for k in range(1, groups):
        near[k - 1].wait_recv()
        there = lax.rem(group + k, groups)
        both = x_ref[there * 2 + side].astype(jnp.float32) + got[k - 1].astype(jnp.float32)
        mine[k - 1] = both.astype(mine.dtype)
        at = groups + k
        far.append(
            send(axis, mine.at[k - 1], far_got.at[k - 1], send_sem.at[at], recv_sem.at[at], across[k - 1])
        )
        far[-1].start()
    near[groups - 1].wait_recv()
    out_ref[...] = x_ref[me].astype(jnp.float32) + got[groups - 1].astype(jnp.float32)
    for k, copy in enumerate(far):
        copy.wait_recv()
        out_ref[...] += far_got[k].astype(jnp.float32)
    for copy in near + far:
        copy.wait_send()


def scatter_rows(x, axis, n, collective_id):
    rows, columns = x.shape
    rows = rows // n
    groups = n // 2
    return pl.pallas_call(
        functools.partial(scatter_kernel, axis, n),
        out_shape=jax.ShapeDtypeStruct((rows, columns), jnp.float32),
        in_specs=[pl.BlockSpec(memory_space=pltpu.VMEM)],
        out_specs=pl.BlockSpec(memory_space=pltpu.VMEM),
        scratch_shapes=[
            pltpu.VMEM((groups, rows, columns), jnp.bfloat16),
            pltpu.VMEM((max(groups - 1, 1), rows, columns), jnp.bfloat16),
            pltpu.VMEM((max(groups - 1, 1), rows, columns), jnp.bfloat16),
            pltpu.SemaphoreType.DMA((n,)),
            pltpu.SemaphoreType.DMA((n,)),
        ],
        compiler_params=pltpu.CompilerParams(collective_id=collective_id, has_side_effects=True),
    )(x.astype(jnp.bfloat16).reshape(n, rows, columns))


def exchange_kernel(axis, n, whole, x_ref, out_ref, send_sem, recv_sem, own_sem):
    me = lax.axis_index(axis)
    peers = [lax.rem(me + k, n) for k in range(1, n)]
    greet(axis, peers)
    own = pltpu.make_async_copy(x_ref if whole else x_ref.at[me], out_ref.at[me], own_sem)
    own.start()
    copies = []
    for k, peer in enumerate(peers):
        src = x_ref if whole else x_ref.at[peer]
        copies.append(send(axis, src, out_ref.at[me], send_sem.at[k], recv_sem.at[k], peer))
        copies[-1].start()
    for copy in copies:
        copy.wait()
    own.wait()


def exchange(x, axis, n, collective_id, whole):
    block = x.shape if whole else x.shape[1:]
    return pl.pallas_call(
        functools.partial(exchange_kernel, axis, n, whole),
        out_shape=jax.ShapeDtypeStruct((n,) + block, x.dtype),
        in_specs=[pl.BlockSpec(memory_space=pltpu.VMEM)],
        out_specs=pl.BlockSpec(memory_space=pltpu.VMEM),
        scratch_shapes=[
            pltpu.SemaphoreType.DMA((n,)),
            pltpu.SemaphoreType.DMA((n,)),
            pltpu.SemaphoreType.DMA,
        ],
        compiler_params=pltpu.CompilerParams(collective_id=collective_id, has_side_effects=True),
    )(x)


def packed(parts, lead):
    flat = jnp.concatenate([p.reshape(lead + (-1,)) for p in parts], -1)
    size = flat.shape[-1]
    room = -(-size // 2048) * 2048
    flat = jnp.pad(flat, [(0, 0)] * len(lead) + [(0, room - size)])
    return flat.reshape(lead + (room // 128, 128))


def layer_norm(rows, gain, shift):
    center = rows - jnp.mean(rows, -1, keepdims=True)
    var = jnp.mean(center * center, -1, keepdims=True)
    return center * lax.rsqrt(var + 1e-05) * gain + shift


def gelu_curve(value):
    return 0.5 * value * (1.0 + jnp.tanh(0.7978845608 * (value + 0.044715 * value * value * value)))


def block_scores(rows_q, keys, start, scale, seq_len):
    block_rows = rows_q.shape[0]
    scores = jnp.einsum("qhe,khe->hqk", rows_q, keys, preferred_element_type=jnp.float32) * scale
    positions = start + jnp.arange(block_rows, dtype=jnp.int32)
    allowed = jnp.arange(seq_len, dtype=jnp.int32)[None, :] <= positions[:, None]
    return (jnp.where(allowed[None], scores, -1e30), allowed)


def attend(query, keys, values):
    seq_len, heads, head_dim = query.shape
    block_rows = min(512, seq_len)
    count = seq_len // block_rows
    scale = 1.0 / math.sqrt(head_dim)
    starts = jnp.arange(count, dtype=jnp.int32) * block_rows

    def one_block(item):
        rows_q, start = item
        scores, allowed = block_scores(rows_q, keys, start, scale, seq_len)
        peak = jnp.max(scores, -1, keepdims=True)
        expo = jnp.exp(scores - peak)
        total = jnp.sum(expo, -1, keepdims=True)
        probs = (expo / total).astype(jnp.bfloat16)
        out = jnp.einsum("hqk,khe->qhe", probs, values, preferred_element_type=jnp.float32).astype(
            jnp.bfloat16
        )
        return (out, (peak + jnp.log(total))[:, :, 0])

    outs, logs = lax.map(one_block, (query.reshape(count, block_rows, heads, head_dim), starts))
    return (outs.reshape(seq_len, heads, head_dim), logs)


def attend_back(query, keys, values, mixed, grad_mixed, log_total):
    seq_len, heads, head_dim = query.shape
    block_rows = min(512, seq_len)
    count = seq_len // block_rows
    scale = 1.0 / math.sqrt(head_dim)
    starts = jnp.arange(count, dtype=jnp.int32) * block_rows
    row_dot = jnp.sum(grad_mixed.astype(jnp.float32) * mixed.astype(jnp.float32), -1)

    def step(carry, item):
        grad_k, grad_v = carry
        rows_q, rows_g, rows_log, rows_dot, start = item
        scores, allowed = block_scores(rows_q, keys, start, scale, seq_len)
        probs = jnp.where(allowed[None], jnp.exp(scores - rows_log[:, :, None]), 0.0)
        probs_low = probs.astype(jnp.bfloat16)
        grad_v = grad_v + jnp.einsum(
            "hqk,qhe->khe", probs_low, rows_g, preferred_element_type=jnp.float32
        )
        grad_p = jnp.einsum("qhe,khe->hqk", rows_g, values, preferred_element_type=jnp.float32)
        grad_s = (probs * (grad_p - jnp.transpose(rows_dot)[:, :, None])).astype(jnp.bfloat16)
        grad_q = (
            jnp.einsum("hqk,khe->qhe", grad_s, keys, preferred_element_type=jnp.float32) * scale
        )
        grad_k = (
            grad_k
            + jnp.einsum("hqk,qhe->khe", grad_s, rows_q, preferred_element_type=jnp.float32) * scale
        )
        return ((grad_k, grad_v), grad_q)

    zeros = jnp.zeros((seq_len, heads, head_dim), jnp.float32)
    items = (
        query.reshape(count, block_rows, heads, head_dim),
        grad_mixed.reshape(count, block_rows, heads, head_dim),
        log_total,
        row_dot.reshape(count, block_rows, heads),
        starts,
    )
    (grad_k, grad_v), grad_qs = lax.scan(step, (zeros, zeros), items)
    return (grad_qs.reshape(seq_len, heads, head_dim), grad_k, grad_v)


def body(dp, tensor, block_in, in_proj, in_bias, out_proj, up_proj, up_bias, down_proj, norm_params, grad_out):
    proj_in = lax.all_gather(in_proj, "dp", axis=1, tiled=True)
    proj_out = gather_rows(out_proj, "dp", dp, 11).reshape((dp,) + out_proj.shape)
    proj_out = proj_out.transpose(1, 0, 2).reshape(out_proj.shape[0], -1)
    small = exchange(packed([norm_params, in_bias, up_bias], ()), "dp", dp, 0, True)
    small = small.reshape(dp, -1)
    ends = [norm_params.size, norm_params.size + in_bias.size]
    ends.append(ends[1] + up_bias.size)
    norms = small[:, : ends[0]].reshape((dp,) + norm_params.shape)
    norms = norms.transpose(1, 0, 2).reshape(6, -1)
    bias_in = small[:, ends[0] : ends[1]].reshape((dp,) + in_bias.shape)
    bias_in = bias_in.transpose(1, 2, 0, 3).reshape(2, in_bias.shape[1], -1)
    bias_up = small[:, ends[1] : ends[2]].reshape((dp,) + up_bias.shape)
    bias_up = bias_up.transpose(1, 0, 2).reshape(up_bias.shape[0], -1)
    norms = norms.astype(jnp.float32)
    gain_one, shift_one, bias_attn, gain_two, shift_two, bias_feed = [norms[i] for i in range(6)]
    heads_here = bias_in.shape[1]
    head_dim = bias_in.shape[2]
    columns = heads_here * head_dim
    normed_one = layer_norm(block_in, gain_one, shift_one).astype(jnp.bfloat16)
    whole_one = gather_rows(normed_one, "tensor", tensor, 1)
    seq_len = whole_one.shape[0]
    projected = jnp.einsum("ld,jdc->jlc", whole_one, proj_in, preferred_element_type=jnp.float32)
    bias_flat = bias_in.astype(jnp.float32).reshape(2, columns)
    query = (
        (projected[0] + bias_flat[0]).astype(jnp.bfloat16).reshape(seq_len, heads_here, head_dim)
    )
    keys = projected[1].astype(jnp.bfloat16).reshape(seq_len, heads_here, head_dim)
    values = (
        (projected[2] + bias_flat[1]).astype(jnp.bfloat16).reshape(seq_len, heads_here, head_dim)
    )
    mixed, log_total = attend(query, keys, values)
    mixed_flat = mixed.reshape(seq_len, columns)
    attn_part = jnp.dot(mixed_flat, proj_out, preferred_element_type=jnp.float32)
    attn_sum = scatter_rows(attn_part, "tensor", tensor, 5)
    middle = block_in + attn_sum + bias_attn
    normed_two = layer_norm(middle, gain_two, shift_two).astype(jnp.bfloat16)
    whole_two = gather_rows(normed_two, "tensor", tensor, 2)
    proj_up = lax.all_gather(up_proj, "dp", axis=0, tiled=True)
    proj_down = lax.all_gather(down_proj, "dp", axis=1, tiled=True)
    hidden_pre = jnp.dot(whole_two, proj_up, preferred_element_type=jnp.float32) + bias_up.astype(
        jnp.float32
    ).reshape(-1)
    hidden = gelu_curve(hidden_pre).astype(jnp.bfloat16)
    feed_part = jnp.dot(hidden, proj_down, preferred_element_type=jnp.float32)
    feed_sum = scatter_rows(feed_part, "tensor", tensor, 6)
    block_out = middle + feed_sum + bias_feed
    grad_low = grad_out.astype(jnp.bfloat16)
    whole_grad = gather_rows(grad_low, "tensor", tensor, 3)
    grad_down = jnp.einsum("lf,ld->fd", hidden, whole_grad, preferred_element_type=jnp.float32)
    grad_hidden = jnp.einsum("ld,fd->lf", whole_grad, proj_down, preferred_element_type=jnp.float32)
    _, curve_back = jax.vjp(gelu_curve, hidden_pre)
    grad_pre = curve_back(grad_hidden)[0]
    grad_upb = jnp.sum(grad_pre, 0).reshape(bias_up.shape)
    grad_pre_low = grad_pre.astype(jnp.bfloat16)
    grad_up = jnp.einsum("ld,lf->df", whole_two, grad_pre_low, preferred_element_type=jnp.float32)
    two_part = jnp.einsum("lf,df->ld", grad_pre_low, proj_up, preferred_element_type=jnp.float32)
    grad_down = grad_down.astype(jnp.bfloat16)
    two_part, grad_down = lax.optimization_barrier((two_part.astype(jnp.bfloat16), grad_down))
    down_sum = lax.psum_scatter(grad_down, "dp", scatter_dimension=1, tiled=True)
    normed_two_grad = scatter_rows(two_part, "tensor", tensor, 7)
    _, norm_back_two = jax.vjp(layer_norm, middle, gain_two, shift_two)
    grad_mid_norm, grad_gain_two, grad_shift_two = norm_back_two(normed_two_grad)
    grad_middle = grad_out + grad_mid_norm
    middle_low = grad_middle.astype(jnp.bfloat16)
    whole_mid = gather_rows(middle_low, "tensor", tensor, 4)
    grad_proj_out = jnp.einsum(
        "lc,ld->cd", mixed_flat, whole_mid, preferred_element_type=jnp.float32
    )
    grad_mixed = jnp.einsum("ld,cd->lc", whole_mid, proj_out, preferred_element_type=jnp.float32)
    grad_mixed = grad_mixed.astype(jnp.bfloat16).reshape(seq_len, heads_here, head_dim)
    grad_q, grad_k, grad_v = attend_back(query, keys, values, mixed, grad_mixed, log_total)
    grad_bias_in = jnp.stack([jnp.sum(grad_q, 0), jnp.sum(grad_v, 0)])
    grad_proj = (
        jnp.stack([grad_q, grad_k, grad_v]).reshape(3, seq_len, columns).astype(jnp.bfloat16)
    )
    grad_in_w = jnp.einsum("ld,jlc->jdc", whole_one, grad_proj, preferred_element_type=jnp.float32)
    one_part = jnp.einsum("jlc,jdc->ld", grad_proj, proj_in, preferred_element_type=jnp.float32)
    one_part, down_sum = lax.optimization_barrier((one_part.astype(jnp.bfloat16), down_sum))
    normed_one_grad = scatter_rows(one_part, "tensor", tensor, 8)
    _, norm_back_one = jax.vjp(layer_norm, block_in, gain_one, shift_one)
    grad_in_norm, grad_gain_one, grad_shift_one = norm_back_one(normed_one_grad)
    grad_in = grad_middle + grad_in_norm
    norm_terms = jnp.stack(
        [
            grad_gain_one,
            grad_shift_one,
            jnp.sum(grad_middle, 0),
            grad_gain_two,
            grad_shift_two,
            jnp.sum(grad_out, 0),
        ]
    )
    pieces = [
        norm_terms.reshape(6, dp, -1).transpose(1, 0, 2),
        grad_bias_in.reshape(in_bias.shape[:2] + (dp, -1)).transpose(2, 0, 1, 3),
        grad_upb.reshape(up_bias.shape[0], dp, -1).transpose(1, 0, 2),
    ]
    pieces = [p.reshape(dp, -1) for p in pieces]
    tiny = jnp.sum(exchange(packed(pieces, (dp,)), "dp", dp, 9, False), 0).reshape(-1)
    grad_in_bias = tiny[ends[0] : ends[1]].reshape(in_bias.shape)
    grad_up_bias = tiny[ends[1] : ends[2]].reshape(up_bias.shape)
    quarter = tiny[: ends[0]].reshape(6, tensor, -1).transpose(1, 0, 2).reshape(tensor, -1)
    width = quarter.shape[1]
    quarter = jnp.sum(exchange(packed([quarter], (tensor,)), "tensor", tensor, 10, False), 0)
    grad_norms = quarter.reshape(-1)[:width].reshape(6, -1)

    blocks = grad_in_w.astype(jnp.bfloat16).reshape(3, dp, -1, columns).transpose(1, 0, 2, 3)
    grad_in_proj = scatter_rows(blocks.reshape(-1, columns), "dp", dp, 12).reshape(in_proj.shape)
    blocks = grad_proj_out.astype(jnp.bfloat16).reshape(columns, dp, -1).transpose(1, 0, 2)
    grad_out_proj = scatter_rows(blocks.reshape(dp * columns, -1), "dp", dp, 13)
    grad_up_proj = scatter_rows(grad_up, "dp", dp, 14)
    grad_down_proj = down_sum.astype(jnp.float32)
    return (
        block_out,
        grad_in,
        grad_in_proj,
        grad_in_bias,
        grad_out_proj,
        grad_up_proj,
        grad_up_bias,
        grad_down_proj,
        grad_norms,
    )


def solution(mesh):
    return jax.shard_map(
        functools.partial(body, mesh.shape["dp"], mesh.shape["tensor"]),
        mesh=mesh,
        in_specs=(
            P(("dp", "tensor"), None),
            P(None, "dp", "tensor"),
            P(None, "tensor", "dp"),
            P("tensor", "dp"),
            P("dp", "tensor"),
            P("tensor", "dp"),
            P("tensor", "dp"),
            P(None, "dp"),
            P(("dp", "tensor"), None),
        ),
        out_specs=(
            P(("dp", "tensor"), None),
            P(("dp", "tensor"), None),
            P(None, "dp", "tensor"),
            P(None, "tensor", "dp"),
            P("tensor", "dp"),
            P("dp", "tensor"),
            P("tensor", "dp"),
            P("tensor", "dp"),
            P(None, ("dp", "tensor")),
        ),
        check_vma=False,
    )
```
